768 devices in a mesh: rep: 96 (over z_hi, x, y), fsdp: 8 (over z_lo, core).
Axes of the slice: x: 4, y: 8, z: 12 (z_hi: 3, z_lo: 4; z = z_hi * 4 + z_lo), core: 2. Of those that a mesh axis runs over, the one named last changes fastest.
Arguments:
- tokens: bfloat16 [98304, 4096], P(('rep', 'fsdp')), may hold values from -6 to 6
- queries: bfloat16 [98304, 2048], P(('rep', 'fsdp')), may hold values from -10 to 10
- rotated_key_rows: bfloat16 [98304, 512], P(('rep', 'fsdp')), may hold values from -3 to 3
- targets: bfloat16 [98304, 2048], P(('rep', 'fsdp')), may hold values from -6 to 6
- value_weights: float32 [4096, 512], P('fsdp'), may hold values from -4 to 4
- momentum: float32 [4096, 512], P('fsdp'), may hold values from -0.6 to 0.6
- first_moment: float32 [96, 4096, 512], P('rep', 'fsdp'), may hold values from -1.8 to 1.8
- second_moment: float32 [96, 4096, 512], P('rep', 'fsdp'), may hold values from 0.02 to 0.5
Outputs:
- new_weights: float32 [4096, 512], P('fsdp')
- new_momentum: float32 [4096, 512], P('fsdp')
The draws below stay inside these ranges and needn't reach their ends.
All inputs are finite; a program needn't handle non-finite values.
Results may differ from the reference program's by a relative error of at most 0.0045.
Values may be sent and summed in bfloat16 or wider, within the bound.
A program may use at most 64 MiB of HBM per device.

```python
import math
import jax
import jax.numpy as jnp
from jax import lax

D = 4096
LOCAL_QUERY_HEADS = 16
LOCAL_KEY_HEADS = 4
HEAD_SIZE = 128
DEVICE_TOKENS = 128
KVW = 512
QW = 2048
RTOK = 1024
REPLICAS = 96
TOTAL_TOKENS = 98304
N_REP = 96
N_FSDP = 8


def attention_couple(key):
    base = jax.random.fold_in(key, 11)
    key_query, key_random_keys = jax.random.split(base, 2)
    queries = jax.random.truncated_normal(key_query, -4.0, 4.0, (TOTAL_TOKENS, LOCAL_QUERY_HEADS, HEAD_SIZE), jnp.float32)
    rotated_key_rows = jax.random.truncated_normal(key_random_keys, -3.0, 3.0, (TOTAL_TOKENS, LOCAL_KEY_HEADS, HEAD_SIZE), jnp.float32)
    return (queries, rotated_key_rows)


def draw_queries(key, part):
    return attention_couple(key)[0].reshape(TOTAL_TOKENS, LOCAL_QUERY_HEADS * HEAD_SIZE).astype(jnp.bfloat16)


def draw_rotated_key_rows(key, part):
    return attention_couple(key)[1].reshape(TOTAL_TOKENS, LOCAL_KEY_HEADS * HEAD_SIZE).astype(jnp.bfloat16)


def shard_levels(key, extent, shards, least, top_value):
    factor_of = 1.0
    for axis_at, shards_of in shards:
        draws = jax.random.uniform(jax.random.fold_in(jax.random.fold_in(key, 6), axis_at), (shards_of,), jnp.float32, least / len(shards), top_value / len(shards))
        factor_of = factor_of * jnp.repeat(jnp.exp(draws), extent[axis_at] // shards_of).reshape((-1,) + (1,) * (len(extent) - 1 - axis_at))
    return factor_of


def scatter_about(rng, extent, width, reach, shards=(), kind=jnp.bfloat16):
    level = shard_levels(rng, extent, shards, -0.22, 0.18) if shards else 1.0
    result = jax.random.normal(rng, extent, jnp.float32) * width * level
    return jnp.minimum(jnp.maximum(result, -reach), reach).astype(kind)


def setup_inputs(seed: int = 0) -> dict:
    streams_of = jax.random.split(jax.random.key(seed), 9)
    return {
        "tokens": scatter_about(streams_of[0], (TOTAL_TOKENS, D), 1.0, 6.0, ((0, 768),)),
        "queries": draw_queries(jax.random.fold_in(streams_of[8], 71), 0),
        "rotated_key_rows": draw_rotated_key_rows(jax.random.fold_in(streams_of[8], 71), 0),
        "targets": scatter_about(streams_of[3], (TOTAL_TOKENS, QW), 1.0, 6.0, ((0, 768),)),
        "value_weights": scatter_about(streams_of[4], (D, KVW), 1.0, 4.0, ((0, 8),), jnp.float32),
        "momentum": scatter_about(streams_of[5], (D, KVW), 0.1, 0.6, ((0, 8),), jnp.float32),
        "first_moment": scatter_about(streams_of[6], (REPLICAS, D, KVW), 0.3, 1.8, ((0, 96), (1, 8)), jnp.float32),
        "second_moment": jnp.clip(jnp.exp(math.log(0.5) - 3.218876 * jax.random.uniform(streams_of[7], (REPLICAS, D, KVW), jnp.float32) ** shard_levels(streams_of[7], (REPLICAS, D, KVW), ((0, 96), (1, 8)), -0.2, 0.2)), 0.02, 0.5),
    }


first_decay = 0.9
second_decay = 0.95
weight_decay = 0.1
inner_rate = 0.05
outer_rate = 0.7
momentum_keep = 0.9
epsilon = 1e-08

def reference(tokens, queries, rotated_key_rows, targets, value_weights, momentum, first_moment, second_moment):
    heads_per_group = LOCAL_QUERY_HEADS // LOCAL_KEY_HEADS
    compact = value_weights.astype(jnp.bfloat16)
    inv_root = 1.0 / math.sqrt(D)
    score_scale = 1.0 / math.sqrt(HEAD_SIZE)
    cot_scale = math.sqrt(D / RTOK)
    causal = jnp.arange(DEVICE_TOKENS)[:, None] >= jnp.arange(DEVICE_TOKENS)[None, :]

    def replica(running, inputs):
        block_tokens, block_query_rows, block_key_rows, block_target_rows, first_old, second_old = inputs
        value_result = (jnp.dot(block_tokens, compact, preferred_element_type=jnp.float32) * inv_root).astype(jnp.bfloat16)
        query_head_count = block_query_rows.reshape(N_FSDP, DEVICE_TOKENS, LOCAL_KEY_HEADS, heads_per_group, HEAD_SIZE).astype(jnp.float32)
        key_head_count = block_key_rows.reshape(N_FSDP, DEVICE_TOKENS, LOCAL_KEY_HEADS, HEAD_SIZE).astype(jnp.float32)
        value_head_count = value_result.reshape(N_FSDP, DEVICE_TOKENS, LOCAL_KEY_HEADS, HEAD_SIZE).astype(jnp.float32)
        scores = jnp.einsum('btgjd,bsgd->bgjts', query_head_count, key_head_count) * score_scale
        scores = jnp.where(causal, scores, -jnp.inf)
        row_top = lax.optimization_barrier(jnp.max(scores, axis=-1, keepdims=True))
        expo = jnp.exp(scores - row_top)
        probs = (expo / lax.optimization_barrier(jnp.sum(expo, axis=-1, keepdims=True))).astype(jnp.bfloat16)
        outputs = jnp.einsum('bgjts,bsgd->btgjd', probs.astype(jnp.float32), value_head_count)
        objective = block_target_rows.reshape(N_FSDP, DEVICE_TOKENS, LOCAL_KEY_HEADS, heads_per_group, HEAD_SIZE).astype(jnp.float32)
        residual_term = ((outputs - objective) * cot_scale).astype(jnp.bfloat16)
        value_grad = jnp.einsum('bgjts,btgjd->bsgd', probs.astype(jnp.float32), residual_term.astype(jnp.float32))
        value_grad = value_grad.astype(jnp.bfloat16).reshape(N_FSDP, DEVICE_TOKENS, KVW)
        partial_value = jnp.einsum('bsi,bsc->bic', block_tokens.reshape(N_FSDP, DEVICE_TOKENS, D).astype(jnp.float32), value_grad.astype(jnp.float32))
        partial_value = lax.optimization_barrier(partial_value.astype(jnp.bfloat16))
        gradient = lax.optimization_barrier(jnp.sum(partial_value.astype(jnp.float32), axis=0)) * inv_root
        first_new = first_decay * first_old + (1.0 - first_decay) * gradient
        second_new = second_decay * second_old + (1.0 - second_decay) * gradient * gradient
        direction = first_new / (jnp.sqrt(second_new) + epsilon) + weight_decay * value_weights
        return (running + direction, None)
    total, _ = lax.scan(replica, jnp.zeros((D, KVW), value_weights.dtype), (tokens.reshape(N_REP, RTOK, D), queries.reshape(N_REP, RTOK, QW), rotated_key_rows.reshape(N_REP, RTOK, KVW), targets.reshape(N_REP, RTOK, QW), first_moment, second_moment))
    mean_direction = total / N_REP
    new_momentum = momentum_keep * momentum + mean_direction
    new_weights = value_weights - outer_rate * inner_rate * (mean_direction + momentum_keep * new_momentum)
    return (new_weights, new_momentum)
```

```python
import math

import jax
import jax.numpy as jnp
from jax import lax
from jax.experimental import pallas as pl
from jax.experimental.pallas import tpu as pltpu
from jax.sharding import PartitionSpec as P

D = 4096
HEAD = 128
NX, NY, NZH, NZL = 4, 8, 3, 4
NREP = NX * NY * NZH
NF = 8
SEQ = 128
KVW = 512
ROWS = 512
GROUPS = 4
HPG = 4
XR = ROWS // NX
YR = XR // NY
MESH = pl.DeviceIdType.MESH
BF = jnp.bfloat16
F32 = jnp.float32

first_decay = 0.9
second_decay = 0.95
weight_decay = 0.1
inner_rate = 0.05
outer_rate = 0.7
momentum_keep = 0.9
epsilon = 1e-08


def rows(start, size):
    return pl.ds(pl.multiple_of(start, size), size)


def kernel(
    tok_h, q_h, k_h, t_h, w_h, m1_h, m2_h, out_ref,
    tok, q, k, t, w, m1, m2,
    wall, tokc, vgall, probs, acc, dirs, xsend, xrecv, xsum, ysend, yrecv, zbuf, mean,
    loc, ws, wr, ts, tr, vs, vr, xs, xr, ys, yr, zs, zr, gs, gr, hs, hr,
):
    r = lax.axis_index("rep")
    f = lax.axis_index("fsdp")
    zh = lax.div(r, NX * NY)
    x = lax.rem(lax.div(r, NY), NX)
    y = lax.rem(r, NY)
    zl = lax.div(f, 2)
    c = lax.rem(f, 2)

    def dev(zh_=zh, x_=x, y_=y, f_=f):
        return {"rep": zh_ * (NX * NY) + x_ * NY + y_, "fsdp": f_}

    sib = f + 1 - 2 * c
    zl_r = lax.rem(zl + 1, NZL)
    zl_l = lax.rem(zl + NZL - 1, NZL)
    zl_o = lax.rem(zl + 2, NZL)
    zpos = zh * NZL + zl
    zp_r = lax.rem(zpos + 1, NZH * NZL)
    zp_l = lax.rem(zpos + NZH * NZL - 1, NZH * NZL)
    right = dev(zh_=lax.div(zp_r, NZL), f_=zl_r * 2 + c)
    left = dev(zh_=lax.div(zp_l, NZL), f_=zl_l * 2 + c)
    sibling = dev(f_=sib)

    loads = []
    for i, (src, dst) in enumerate(
        [(w_h, w), (tok_h, tok), (q_h, q), (k_h, k), (t_h, t), (m1_h, m1), (m2_h, m2)]
    ):
        cp = pltpu.make_async_copy(src, dst, loc.at[i])
        cp.start()
        loads.append(cp)

    barrier = pltpu.get_barrier_semaphore()
    peers = [right, left]
    peers += [dev(f_=lax.rem(f + d, NF)) for d in range(1, NF)]
    peers += [dev(x_=lax.rem(x + d, NX)) for d in range(1, NX)]
    peers += [dev(y_=lax.rem(y + d, NY)) for d in range(1, NY)]
    peers += [dev(zh_=lax.rem(zh + d, NZH)) for d in range(1, NZH)]
    for p in peers:
        pl.semaphore_signal(barrier, inc=1, device_id=p, device_id_type=MESH)

    loads[0].wait()
    wall[f] = w[...].astype(BF)
    pl.semaphore_wait(barrier, len(peers))

    def remote(src, dst, ss, rs, to):
        return pltpu.make_async_remote_copy(
            src_ref=src, dst_ref=dst, send_sem=ss, recv_sem=rs, device_id=to, device_id_type=MESH
        )

    H = ROWS // 2

    def whalf(slot, h):
        return wall.at[slot, pl.ds(h * H, H)]

    sends = []

    def go(cp):
        cp.start()
        sends.append(cp)

    go(remote(whalf(f, 0), whalf(f, 0), ws.at[0], wr.at[0], right))
    go(remote(whalf(f, 1), whalf(f, 1), ws.at[1], wr.at[1], left))
    go(remote(whalf(f, 1), whalf(f, 1), ws.at[2], wr.at[2], right))
    go(remote(whalf(f, 0), whalf(f, 0), ws.at[3], wr.at[3], left))
    go(remote(wall.at[f], wall.at[f], ws.at[4], wr.at[4], sibling))

    f_l = zl_l * 2 + c
    f_r = zl_r * 2 + c
    f_o = zl_o * 2 + c

    loads[2].wait()
    loads[3].wait()
    causal = lax.broadcasted_iota(jnp.int32, (SEQ, SEQ), 0) >= lax.broadcasted_iota(
        jnp.int32, (SEQ, SEQ), 1
    )
    score_scale = 1.0 / math.sqrt(HEAD)

    def scores_of(g):
        kg = k[:, g * HEAD : (g + 1) * HEAD]
        for j in range(HPG):
            h = g * HPG + j
            s = lax.dot_general(
                q[:, h * HEAD : (h + 1) * HEAD], kg, (((1,), (1,)), ((), ())),
                preferred_element_type=F32,
            )
            s = jnp.where(causal, s * score_scale, -jnp.inf)
            e = jnp.exp(s - jnp.max(s, axis=-1, keepdims=True))
            p = e / jnp.sum(e, axis=-1, keepdims=True)
            probs[g, j * SEQ : (j + 1) * SEQ, :] = p.astype(BF)

    loads[1].wait()

    def term(slot):
        return jnp.dot(
            tok[:, rows(slot * ROWS, ROWS)], wall[slot], preferred_element_type=F32
        )

    acc[...] = term(f)
    for g in range(GROUPS):
        scores_of(g)

    def got(buf, rs):
        remote(buf, buf, ws.at[0], rs, sibling).wait_recv()

    got(wall.at[sib], wr.at[4])
    acc[...] += term(sib)

    got(whalf(f_l, 0), wr.at[0])
    go(remote(whalf(f_l, 0), whalf(f_l, 0), ws.at[5], wr.at[5], right))
    got(whalf(f_r, 1), wr.at[1])
    go(remote(whalf(f_r, 1), whalf(f_r, 1), ws.at[6], wr.at[6], left))
    got(whalf(f_l, 1), wr.at[2])
    go(remote(wall.at[f_l], wall.at[f_l], ws.at[7], wr.at[7], sibling))
    got(whalf(f_r, 0), wr.at[3])
    go(remote(wall.at[f_r], wall.at[f_r], ws.at[8], wr.at[8], sibling))

    tsends = []
    order = [1, 2, 3]
    for n, dz in enumerate(order):
        for cc in range(2):
            to = lax.rem(zl + dz, NZL) * 2 + lax.rem(c + cc, 2)
            i = n * 2 + cc
            cp = remote(
                tok.at[:, rows(to * ROWS, ROWS)], tokc.at[rows(f * SEQ, SEQ)],
                ts.at[i], tr.at[i], dev(f_=to),
            )
            cp.start()
            tsends.append(cp)
    cp = remote(
        tok.at[:, rows(sib * ROWS, ROWS)], tokc.at[rows(f * SEQ, SEQ)], ts.at[6], tr.at[6], sibling
    )
    cp.start()
    tsends.append(cp)
    tokc[rows(f * SEQ, SEQ), :] = tok[:, rows(f * ROWS, ROWS)]

    acc[...] += term(f_l)
    acc[...] += term(f_r)
    got(wall.at[zl_l * 2 + 1 - c], wr.at[7])
    acc[...] += term(zl_l * 2 + 1 - c)
    got(wall.at[zl_r * 2 + 1 - c], wr.at[8])
    acc[...] += term(zl_r * 2 + 1 - c)
    got(whalf(f_o, 0), wr.at[5])
    go(remote(whalf(f_o, 0), whalf(f_o, 0), ws.at[9], wr.at[9], sibling))
    got(whalf(f_o, 1), wr.at[6])
    go(remote(whalf(f_o, 1), whalf(f_o, 1), ws.at[10], wr.at[10], sibling))
    acc[...] += term(f_o)
    f_os = zl_o * 2 + 1 - c
    got(whalf(f_os, 0), wr.at[9])
    got(whalf(f_os, 1), wr.at[10])
    acc[...] += term(f_os)

    inv_root = 1.0 / math.sqrt(D)
    cot_scale = math.sqrt(D / (SEQ * NF))
    loads[4].wait()
    for g in range(GROUPS):
        cols = slice(g * HEAD, (g + 1) * HEAD)
        v = (acc[:, cols] * inv_root).astype(BF)
        o = jnp.dot(probs[g], v, preferred_element_type=F32)
        tg = jnp.concatenate(
            [t[:, (g * HPG + j) * HEAD : (g * HPG + j + 1) * HEAD] for j in range(HPG)], axis=0
        )
        res = ((o - tg.astype(F32)) * cot_scale).astype(BF)
        vg = lax.dot_general(probs[g], res, (((0,), (0,)), ((), ())), preferred_element_type=F32)
        vgall[rows(f * SEQ, SEQ), cols] = vg.astype(BF)

    def vslot(s):
        return vgall.at[rows(s * SEQ, SEQ)]

    def vcopy(slot, i, to):
        return remote(vslot(slot), vslot(slot), vs.at[i], vr.at[i], to)

    right_f = dev(f_=jnp.minimum(f + 2, NF - 2 + c))
    left_f = dev(f_=jnp.maximum(f - 2, c))
    vcopy(f, 6, sibling).start()

    @pl.when(zl < NZL - 1)
    def _():
        vcopy(f, 0, right_f).start()

    @pl.when(zl > 0)
    def _():
        vcopy(f, 3, left_f).start()

    for h in range(1, NZL):
        @pl.when(zl >= h)
        def _():
            slot = f - 2 * h
            vcopy(slot, h - 1, sibling).wait_recv()
            if h < NZL - 1:
                @pl.when(zl < NZL - 1)
                def _():
                    vcopy(slot, h, right_f).start()
            vcopy(slot, 6 + h, sibling).start()

        @pl.when(zl + h < NZL)
        def _():
            slot = f + 2 * h
            vcopy(slot, 3 + h - 1, sibling).wait_recv()
            if h < NZL - 1:
                @pl.when(zl > 0)
                def _():
                    vcopy(slot, 3 + h, left_f).start()
            vcopy(slot, 9 + h, sibling).start()

    vcopy(sib, 6, sibling).wait_recv()
    for h in range(1, NZL):
        @pl.when(zl >= h)
        def _():
            vcopy(sib - 2 * h, 6 + h, sibling).wait_recv()

        @pl.when(zl + h < NZL)
        def _():
            vcopy(sib + 2 * h, 9 + h, sibling).wait_recv()

    for n, dz in enumerate(order):
        for cc in range(2):
            frm = lax.rem(zl + NZL - dz, NZL) * 2 + lax.rem(c + cc, 2)
            i = n * 2 + cc
            remote(
                tokc.at[rows(frm * SEQ, SEQ)], tokc.at[rows(frm * SEQ, SEQ)],
                ts.at[i], tr.at[i], sibling,
            ).wait_recv()
    remote(
        tokc.at[rows(sib * SEQ, SEQ)], tokc.at[rows(sib * SEQ, SEQ)], ts.at[6], tr.at[6], sibling
    ).wait_recv()

    loads[5].wait()
    loads[6].wait()

    def direction(q_):
        at = rows(q_ * XR, XR)
        grad = lax.dot_general(
            tokc[:, at], vgall[...], (((0,), (0,)), ((), ())), preferred_element_type=F32
        ) * inv_root
        fn = first_decay * m1[at, :] + (1.0 - first_decay) * grad
        sn = second_decay * m2[at, :] + (1.0 - second_decay) * grad * grad
        return fn / (jnp.sqrt(sn) + epsilon)

    xorder = [2, 1, 3]
    xsends = []
    for d in xorder:
        px = lax.rem(x + d, NX)
        xsend[d - 1] = direction(px).astype(BF)
        cp = remote(xsend.at[d - 1], xrecv.at[d - 1], xs.at[d - 1], xr.at[d - 1], dev(x_=px))
        cp.start()
        xsends.append(cp)
    xsum[...] = direction(x)
    for d in xorder:
        remote(xrecv.at[d - 1], xrecv.at[d - 1], xs.at[d - 1], xr.at[d - 1], sibling).wait_recv()
    total = xsum[...]
    for d in range(1, NX):
        total = total + xrecv[d - 1].astype(F32)
    xsum[...] = total
    ysend[...] = total.astype(BF)

    yorder = [4, 3, 5, 2, 6, 1, 7]
    for d in yorder:
        py = lax.rem(y + d, NY)
        go(remote(ysend.at[rows(py * YR, YR)], yrecv.at[d - 1], ys.at[d - 1], yr.at[d - 1], dev(y_=py)))
    for d in yorder:
        remote(yrecv.at[d - 1], yrecv.at[d - 1], ys.at[d - 1], yr.at[d - 1], sibling).wait_recv()
    total = xsum[rows(y * YR, YR), :]
    for d in range(1, NY):
        total = total + yrecv[d - 1].astype(F32)

    zbuf[zh] = total.astype(BF)
    for d in range(1, NZH):
        go(remote(zbuf.at[zh], zbuf.at[zh], zs.at[d - 1], zr.at[d - 1], dev(zh_=lax.rem(zh + d, NZH))))
    for d in range(1, NZH):
        frm = lax.rem(zh + NZH - d, NZH)
        remote(zbuf.at[frm], zbuf.at[frm], zs.at[d - 1], zr.at[d - 1], sibling).wait_recv()
    total = zbuf[0].astype(F32)
    for i in range(1, NZH):
        total = total + zbuf[i].astype(F32)

    mine = rows(x * XR + y * YR, YR)
    mean[mine, :] = (total * (1.0 / NREP)).astype(BF)
    for d in yorder:
        py = lax.rem(y + d, NY)
        go(remote(mean.at[mine], mean.at[mine], gs.at[d - 1], gr.at[d - 1], dev(y_=py)))
    for d in yorder:
        frm = rows(x * XR + lax.rem(y + NY - d, NY) * YR, YR)
        remote(mean.at[frm], mean.at[frm], gs.at[d - 1], gr.at[d - 1], sibling).wait_recv()
    block = rows(x * XR, XR)
    for d in xorder:
        px = lax.rem(x + d, NX)
        go(remote(mean.at[block], mean.at[block], hs.at[d - 1], hr.at[d - 1], dev(x_=px)))
    for d in xorder:
        frm = rows(lax.rem(x + NX - d, NX) * XR, XR)
        remote(mean.at[frm], mean.at[frm], hs.at[d - 1], hr.at[d - 1], sibling).wait_recv()
    out_ref[...] = mean[...]

    for cp in sends + tsends + xsends:
        cp.wait_send()
    vcopy(f, 6, sibling).wait_send()

    @pl.when(zl < NZL - 1)
    def _():
        vcopy(f, 0, right_f).wait_send()

    @pl.when(zl > 0)
    def _():
        vcopy(f, 3, left_f).wait_send()

    for h in range(1, NZL):
        @pl.when(zl >= h)
        def _():
            slot = f - 2 * h
            if h < NZL - 1:
                @pl.when(zl < NZL - 1)
                def _():
                    vcopy(slot, h, right_f).wait_send()
            vcopy(slot, 6 + h, sibling).wait_send()

        @pl.when(zl + h < NZL)
        def _():
            slot = f + 2 * h
            if h < NZL - 1:
                @pl.when(zl > 0)
                def _():
                    vcopy(slot, 3 + h, left_f).wait_send()
            vcopy(slot, 9 + h, sibling).wait_send()


def step(tokens, queries, keys, targets, weights, m1, m2):
    dma = pltpu.SemaphoreType.DMA
    V = pltpu.VMEM
    return pl.pallas_call(
        kernel,
        out_shape=jax.ShapeDtypeStruct((ROWS, KVW), BF),
        in_specs=[pl.BlockSpec(memory_space=pl.ANY)] * 7,
        out_specs=pl.BlockSpec(memory_space=pltpu.VMEM),
        scratch_shapes=[
            V((SEQ, D), BF), V((SEQ, 2048), BF), V((SEQ, KVW), BF), V((SEQ, 2048), BF),
            V((ROWS, KVW), F32), V((ROWS, KVW), F32), V((ROWS, KVW), F32),
            V((NF, ROWS, KVW), BF), V((NF * SEQ, ROWS), BF), V((NF * SEQ, KVW), BF),
            V((GROUPS, HPG * SEQ, SEQ), BF), V((SEQ, KVW), F32), V((8, 128), F32),
            V((NX - 1, XR, KVW), BF), V((NX - 1, XR, KVW), BF), V((XR, KVW), F32),
            V((XR, KVW), BF), V((NY - 1, YR, KVW), BF), V((NZH, YR, KVW), BF), V((ROWS, KVW), BF),
            dma((7,)), dma((11,)), dma((11,)), dma((7,)), dma((7,)), dma((13,)), dma((13,)),
            dma((3,)), dma((3,)), dma((7,)), dma((7,)), dma((2,)), dma((2,)),
            dma((7,)), dma((7,)), dma((3,)), dma((3,)),
        ],
        compiler_params=pltpu.CompilerParams(
            collective_id=0, has_side_effects=True, vmem_limit_bytes=58 << 20
        ),
    )(tokens, queries, keys, targets, weights, m1, m2)


def per_device(
    tokens, queries, rotated_key_rows, targets, value_weights, momentum, first_moment, second_moment
):
    mean = step(
        tokens, queries, rotated_key_rows, targets, value_weights, first_moment[0], second_moment[0]
    )
    mean_direction = mean.astype(F32) + weight_decay * value_weights
    new_momentum = momentum_keep * momentum + mean_direction
    new_weights = value_weights - outer_rate * inner_rate * (
        mean_direction + momentum_keep * new_momentum
    )
    return (new_weights, new_momentum)


def solution(mesh):
    in_specs = (
        P(("rep", "fsdp"), None),
        P(("rep", "fsdp"), None),
        P(("rep", "fsdp"), None),
        P(("rep", "fsdp"), None),
        P("fsdp", None),
        P("fsdp", None),
        P("rep", "fsdp", None),
        P("rep", "fsdp", None),
    )
    out_specs = (P("fsdp", None), P("fsdp", None))
    return jax.shard_map(
        per_device, mesh=mesh, in_specs=in_specs, out_specs=out_specs, check_vma=False
    )
```

```python
import math

import jax
import jax.numpy as jnp
from jax import lax
from jax.experimental import pallas as pl
from jax.experimental.pallas import tpu as pltpu
from jax.sharding import PartitionSpec as P

D = 4096
HEAD = 128
NX, NY, NZH, NZL = 4, 8, 3, 4
NREP = NX * NY * NZH
NF = 8
SEQ = 128
KVW = 512
ROWS = 512
GROUPS = 4
HPG = 4
XR = ROWS // NX
YR = XR // NY
MESH = pl.DeviceIdType.MESH
BF = jnp.bfloat16
F32 = jnp.float32

first_decay = 0.9
second_decay = 0.95
weight_decay = 0.1
inner_rate = 0.05
outer_rate = 0.7
momentum_keep = 0.9
epsilon = 1e-08


def rows(start, size):
    return pl.ds(pl.multiple_of(start, size), size)


HALF = ROWS // 2
RA = ROWS * 3 // 4
XS = RA // NX
YS = (ROWS - RA) // NY
CH = KVW // 2
CA = KVW * 3 // 4
CB = KVW - CA
BR = ROWS // NY
PW = ROWS // 2


def kernel(
    tok_h, q_h, k_h, t_h, w_h, m1_h, m2_h, out_ref,
    tok, q, k, t, w, m1, m2,
    wall, tokc, vgall, probs, acc, dirs, dsend_a, dsend_b,
    recv1a, recv1b, sum_a, sum_b, send_a, send_b, recv2a, recv2b, zbuf, mean_a, mean_b,
    loc, lt, wz, wx, wy, wd, ts, vs, r1a, r1b, r2a, r2b, rz, g1a, g1b, g2a, g2b,
):
    r = lax.axis_index("rep")
    f = lax.axis_index("fsdp")
    zh = lax.div(r, NX * NY)
    x = lax.rem(lax.div(r, NY), NX)
    y = lax.rem(r, NY)
    zl = lax.div(f, 2)
    c = lax.rem(f, 2)

    def dev(zh_=zh, x_=x, y_=y, f_=f):
        return {"rep": zh_ * (NX * NY) + x_ * NY + y_, "fsdp": f_}

    def along(d):
        zp = lax.rem(zh * NZL + zl + d + NZH * NZL, NZH * NZL)
        return dev(zh_=lax.div(zp, NZL), f_=lax.rem(zp, NZL) * 2 + c)

    sib = f + 1 - 2 * c
    sibling = dev(f_=sib)
    right, left, right2, left2 = along(1), along(-1), along(2), along(-2)
    x_r, x_l = dev(x_=lax.rem(x + 1, NX)), dev(x_=lax.rem(x + NX - 1, NX))
    y_r, y_l = dev(y_=lax.rem(y + 1, NY)), dev(y_=lax.rem(y + NY - 1, NY))

    loads = [pltpu.make_async_copy(w_h, w, loc.at[0])]
    loads[0].start()

    barrier = pltpu.get_barrier_semaphore()
    peers = [right, left, right2, left2]
    peers += [dev(f_=lax.rem(f + d, NF)) for d in range(1, NF)]
    peers += [dev(x_=lax.rem(x + d, NX)) for d in range(1, NX)]
    peers += [dev(y_=lax.rem(y + d, NY)) for d in range(1, NY)]
    peers += [dev(zh_=lax.rem(zh + d, NZH)) for d in range(1, NZH)]
    for p in peers:
        pl.semaphore_signal(barrier, inc=1, device_id=p, device_id_type=MESH)

    tloads = []
    for j in range(D // PW):
        ct = pltpu.make_async_copy(tok_h.at[:, pl.ds(j * PW, PW)], tok.at[j], lt.at[j])
        ct.start()
        tloads.append(ct)
    for i, (src, dst) in enumerate([(q_h, q), (k_h, k), (t_h, t), (m1_h, m1), (m2_h, m2)]):
        cp = pltpu.make_async_copy(src, dst, loc.at[i + 1])
        cp.start()
        loads.append(cp)

    loads[0].wait()
    wall[f] = w[...].astype(BF)
    pl.semaphore_wait(barrier, len(peers))

    def remote(src, dst, sem, i, to):
        return pltpu.make_async_remote_copy(
            src_ref=src, dst_ref=dst, send_sem=sem.at[0, i], recv_sem=sem.at[1, i],
            device_id=to, device_id_type=MESH,
        )

    sends = []

    def go(ref, sem, i, to, dst=None):
        cp = remote(ref, ref if dst is None else dst, sem, i, to)
        cp.start()
        sends.append(cp)

    def got(ref, sem, i):
        remote(ref, ref, sem, i, sibling).wait_recv()

    f_l = lax.rem(zl + NZL - 1, NZL) * 2 + c
    f_r = lax.rem(zl + 1, NZL) * 2 + c
    f_o = lax.rem(zl + 2, NZL) * 2 + c
    slots = [f_l, f_r, f_o]

    def wa(s, p, h=None):
        if h is None:
            return wall.at[s, rows(p * XS, XS)]
        return wall.at[s, rows(p * XS + h * (XS // 2), XS // 2)]

    def wb(s, p):
        return wall.at[s, rows(RA + p * YS, YS)]

    def at_x(d):
        return lax.rem(x + d + NX, NX)

    def at_y(d):
        return lax.rem(y + d + NY, NY)

    far_y = [4, 3, 5, 2, 6, 1, 7]
    far_x = [2, 1, 3]

    go(wa(f, x), wz, 0, right)
    go(wb(f, y), wz, 1, right)
    go(wa(f, x), wz, 2, left)
    go(wb(f, y), wz, 3, left)
    go(wa(f, x), wz, 4, right2)
    go(wb(f, y), wz, 5, left2)
    go(wall.at[f], wd, 0, sibling)

    px = lax.div(x, 2)
    pairs = [1 - px, px]
    TH = SEQ // 2

    def tparts(n):
        to = lax.rem(f + n, NF)
        frm = lax.rem(f + NF - n, NF)
        whole = (tok.at[2 * to + pairs[0]], tokc.at[pairs[0], rows(f * SEQ, SEQ)],
                 tokc.at[pairs[0], rows(frm * SEQ, SEQ)])
        halves = [
            (tok.at[2 * to + pairs[1], pl.ds(h * TH, TH)],
             tokc.at[pairs[1], rows(f * SEQ + h * TH, TH)],
             tokc.at[pairs[1], rows(frm * SEQ + h * TH, TH)])
            for h in range(2)
        ]
        return [whole] + halves

    def tsend(part):
        for n in range(1, NF):
            src, dst, _ = tparts(n)[part]
            go(src, ts, part * 7 + n - 1, dev(f_=lax.rem(f + n, NF)), dst=dst)

    def tgot(part):
        for n in range(1, NF):
            got(tparts(n)[part][2], ts, part * 7 + n - 1)

    for ct in tloads:
        ct.wait()
    tsend(0)
    tsend(1)
    for m in range(2):
        tokc[m, rows(f * SEQ, SEQ), :] = tok[2 * f + m]

    loads[1].wait()
    loads[2].wait()
    causal = lax.broadcasted_iota(jnp.int32, (SEQ, SEQ), 0) >= lax.broadcasted_iota(
        jnp.int32, (SEQ, SEQ), 1
    )
    score_scale = 1.0 / math.sqrt(HEAD)

    def scores_of(g):
        kg = k[:, g * HEAD : (g + 1) * HEAD]
        for j in range(HPG):
            h = g * HPG + j
            s = lax.dot_general(
                q[:, h * HEAD : (h + 1) * HEAD], kg, (((1,), (1,)), ((), ())),
                preferred_element_type=F32,
            )
            s = jnp.where(causal, s * score_scale, -jnp.inf)
            e = jnp.exp(s - jnp.max(s, axis=-1, keepdims=True))
            p = e / jnp.sum(e, axis=-1, keepdims=True)
            probs[g, j * SEQ : (j + 1) * SEQ, :] = p.astype(BF)

    for g in range(2):
        scores_of(g)

    for n, s in enumerate(slots):
        got(wa(s, x), wz, 2 * n)
        go(wa(s, x), wx, n, x_r)
        go(wa(s, x), wx, 3 + n, x_l)
        got(wb(s, y), wz, 2 * n + 1)
        for d in far_y:
            go(wb(s, y), wy, n * 7 + d - 1, dev(y_=at_y(d)))

    def term(slot, h):
        return jnp.dot(
            tok[2 * slot + h], wall[slot, h * HALF : (h + 1) * HALF, :],
            preferred_element_type=F32,
        )

    acc[...] = term(f, 0) + term(f, 1)
    scores_of(2)
    for n, s in enumerate(slots):
        got(wa(s, at_x(-1)), wx, n)
        go(wa(s, at_x(-1), 0), wx, 6 + n, x_r)
        got(wa(s, at_x(1)), wx, 3 + n)
        go(wa(s, at_x(1), 1), wx, 9 + n, x_l)
    scores_of(3)
    got(wall.at[sib], wd, 0)
    acc[...] += term(sib, 0) + term(sib, 1)

    def part(s, h):
        return wall.at[s, pl.ds(0, RA)] if h == 0 else wall.at[s, pl.ds(RA, ROWS - RA)]

    for n, s in enumerate(slots):
        for d in far_y:
            got(wb(s, at_y(-d)), wy, n * 7 + d - 1)
        go(part(s, 1), wd, 4 + n, sibling)
    for n, s in enumerate(slots):
        got(wa(s, at_x(2), 0), wx, 6 + n)
        got(wa(s, at_x(2), 1), wx, 9 + n)
        go(part(s, 0), wd, 1 + n, sibling)
        acc[...] += term(s, 0) + term(s, 1)
    for n, s in enumerate(slots):
        o = s + 1 - 2 * c
        got(part(o, 1), wd, 4 + n)
        got(part(o, 0), wd, 1 + n)
        acc[...] += term(o, 0) + term(o, 1)

    inv_root = 1.0 / math.sqrt(D)
    cot_scale = math.sqrt(D / (SEQ * NF))
    loads[3].wait()

    def value_grad_of(g):
        cols = slice(g * HEAD, (g + 1) * HEAD)
        v = (acc[:, cols] * inv_root).astype(BF)
        o = jnp.dot(probs[g], v, preferred_element_type=F32)
        tg = jnp.concatenate(
            [t[:, (g * HPG + j) * HEAD : (g * HPG + j + 1) * HEAD] for j in range(HPG)], axis=0
        )
        res = ((o - tg.astype(F32)) * cot_scale).astype(BF)
        vg = lax.dot_general(probs[g], res, (((0,), (0,)), ((), ())), preferred_element_type=F32)
        vgall[g // 2, rows(f * SEQ, SEQ), (g % 2) * HEAD : (g % 2 + 1) * HEAD] = vg.astype(BF)

    def vcopy(slot, i, ch, to):
        ref = vgall.at[ch, rows(slot * SEQ, SEQ)]
        return remote(ref, ref, vs, ch * 13 + i, to)

    right_f = dev(f_=jnp.minimum(f + 2, NF - 2 + c))
    left_f = dev(f_=jnp.maximum(f - 2, c))

    def own_copies(ch, act):
        act(vcopy(f, 6, ch, sibling))

        @pl.when(zl < NZL - 1)
        def _():
            act(vcopy(f, 0, ch, right_f))

        @pl.when(zl > 0)
        def _():
            act(vcopy(f, 3, ch, left_f))

    def relay(h, ch, act, wait):
        @pl.when(zl >= h)
        def _():
            slot = f - 2 * h
            if wait:
                vcopy(slot, h - 1, ch, sibling).wait_recv()
            if h < NZL - 1:
                @pl.when(zl < NZL - 1)
                def _():
                    act(vcopy(slot, h, ch, right_f))
            act(vcopy(slot, 6 + h, ch, sibling))

        @pl.when(zl + h < NZL)
        def _():
            slot = f + 2 * h
            if wait:
                vcopy(slot, 3 + h - 1, ch, sibling).wait_recv()
            if h < NZL - 1:
                @pl.when(zl > 0)
                def _():
                    act(vcopy(slot, 3 + h, ch, left_f))
            act(vcopy(slot, 9 + h, ch, sibling))

    def start(cp):
        cp.start()

    def sent(cp):
        cp.wait_send()

    for ch in range(2):
        value_grad_of(2 * ch)
        value_grad_of(2 * ch + 1)
        own_copies(ch, start)
    for h in range(1, NZL):
        for ch in range(2):
            relay(h, ch, start, True)
    tsend(2)

    def sibling_got(ch):
        vcopy(sib, 6, ch, sibling).wait_recv()
        for h in range(1, NZL):
            @pl.when(zl >= h)
            def _():
                vcopy(sib - 2 * h, 6 + h, ch, sibling).wait_recv()

            @pl.when(zl + h < NZL)
            def _():
                vcopy(sib + 2 * h, 9 + h, ch, sibling).wait_recv()

    for ch in range(2):
        sibling_got(ch)
    loads[4].wait()
    loads[5].wait()

    A, B = slice(0, CA), slice(CA, KVW)

    def direction(m, e):
        n = 2 * m + e
        at = rows(n * XR, XR)
        for ch in range(2):
            cols = slice(ch * CH, (ch + 1) * CH)
            grad = lax.dot_general(
                tokc[m, :, rows(e * XR, XR)], vgall[ch], (((0,), (0,)), ((), ())),
                preferred_element_type=F32,
            ) * inv_root
            fn = first_decay * m1[at, cols] + (1.0 - first_decay) * grad
            sn = second_decay * m2[at, cols] + (1.0 - second_decay) * grad * grad
            dirs[at, cols] = fn / (jnp.sqrt(sn) + epsilon)
        d = dirs[at, :]
        dsend_a[at, :] = d[:, A].astype(BF)
        dsend_b[at, :] = d[:, B].astype(BF)
        return n

    b = lax.rem(x, 2)
    ysends = []
    for i, (m, e) in enumerate([(1 - px, b), (1 - px, 1 - b), (px, 1 - b), (px, b)]):
        if i == 0:
            tgot(0)
        if i == 2:
            tgot(1)
            tgot(2)
        n = direction(m, e)
        if i < 3:
            go(dsend_a.at[rows(n * XR, XR)], r1a, i, dev(x_=n), dst=recv1a.at[i])
        for u in range(2):
            to = 2 * n + u
            j = lax.rem(to - y + NY, NY)
            cp = remote(dsend_b.at[rows(to * BR, BR)], recv1b.at[j], r1b, j, dev(y_=to))
            ysends.append((to, cp))

            @pl.when(to != y)
            def _():
                cp.start()

    for i in range(3):
        got(recv1a.at[i], r1a, i)
    total = dirs[rows(x * XR, XR), A]
    for i in range(3):
        total = total + recv1a[i].astype(F32)
    sum_a[...] = total
    send_a[...] = total.astype(BF)
    for d in far_y:
        go(send_a.at[rows(at_y(d) * YR, YR)], r2a, d - 1, dev(y_=at_y(d)), dst=recv2a.at[d - 1])
    for d in range(1, NY):
        got(recv1b.at[d], r1b, d)
    total = dirs[rows(y * BR, BR), B]
    for d in range(1, NY):
        total = total + recv1b[d].astype(F32)
    sum_b[...] = total
    send_b[...] = total.astype(BF)
    for d in far_x:
        go(send_b.at[rows(at_x(d) * YR, YR)], r2b, d - 1, dev(x_=at_x(d)), dst=recv2b.at[d - 1])
    for d in range(1, NY):
        got(recv2a.at[d - 1], r2a, d - 1)
    total = sum_a[rows(y * YR, YR), :]
    for d in range(1, NY):
        total = total + recv2a[d - 1].astype(F32)
    zbuf[zh, :, A] = total.astype(BF)
    for d in range(1, NX):
        got(recv2b.at[d - 1], r2b, d - 1)
    total = sum_b[rows(x * YR, YR), :]
    for d in range(1, NX):
        total = total + recv2b[d - 1].astype(F32)
    zbuf[zh, :, B] = total.astype(BF)

    for d in range(1, NZH):
        go(zbuf.at[zh], rz, d - 1, dev(zh_=lax.rem(zh + d, NZH)))
    for d in range(1, NZH):
        got(zbuf.at[lax.rem(zh + NZH - d, NZH)], rz, d - 1)

    def spot_a(x_, y_):
        return mean_a.at[rows(x_ * XR + y_ * YR, YR)]

    def spot_b(x_, y_):
        return mean_b.at[rows(y_ * BR + x_ * YR, YR)]

    total = zbuf[0].astype(F32)
    for z in range(1, NZH):
        total = total + zbuf[z].astype(F32)
    piece = (total * (1.0 / NREP)).astype(BF)
    mean_a[rows(x * XR + y * YR, YR), :] = piece[:, A]
    for d in far_y:
        go(spot_a(x, y), g1a, d - 1, dev(y_=at_y(d)))
    mean_b[rows(y * BR + x * YR, YR), :] = piece[:, B]
    for d in far_x:
        go(spot_b(x, y), g1b, d - 1, dev(x_=at_x(d)))
    for d in far_x:
        got(spot_b(at_x(-d), y), g1b, d - 1)
    for d in far_y:
        go(mean_b.at[rows(y * BR, BR)], g2b, d - 1, dev(y_=at_y(d)))
    for d in far_y:
        got(spot_a(x, at_y(-d)), g1a, d - 1)
    for d in far_x:
        go(mean_a.at[rows(x * XR, XR)], g2a, d - 1, dev(x_=at_x(d)))
    for d in far_y:
        got(mean_b.at[rows(at_y(-d) * BR, BR)], g2b, d - 1)
    out_ref[:, B] = mean_b[...]
    for d in far_x:
        got(mean_a.at[rows(at_x(-d) * XR, XR)], g2a, d - 1)
    out_ref[:, A] = mean_a[...]

    for cp in sends:
        cp.wait_send()
    for to, cp in ysends:
        @pl.when(to != y)
        def _():
            cp.wait_send()
    for ch in range(2):
        own_copies(ch, sent)
        for h in range(1, NZL):
            relay(h, ch, sent, False)


def step(tokens, queries, keys, targets, weights, m1, m2):
    def dma(n):
        return pltpu.SemaphoreType.DMA((2, n))

    V = pltpu.VMEM
    return pl.pallas_call(
        kernel,
        out_shape=jax.ShapeDtypeStruct((ROWS, KVW), BF),
        in_specs=[pl.BlockSpec(memory_space=pl.ANY)] * 7,
        out_specs=pl.BlockSpec(memory_space=pltpu.VMEM),
        scratch_shapes=[
            V((D // PW, SEQ, PW), BF), V((SEQ, 2048), BF), V((SEQ, KVW), BF), V((SEQ, 2048), BF),
            V((ROWS, KVW), F32), V((ROWS, KVW), F32), V((ROWS, KVW), F32),
            V((NF, ROWS, KVW), BF), V((2, NF * SEQ, PW), BF), V((2, NF * SEQ, CH), BF),
            V((GROUPS, HPG * SEQ, SEQ), BF), V((SEQ, KVW), F32),
            V((ROWS, KVW), F32), V((ROWS, CA), BF), V((ROWS, CB), BF),
            V((NX - 1, XR, CA), BF), V((NY, BR, CB), BF),
            V((XR, CA), F32), V((BR, CB), F32), V((XR, CA), BF), V((BR, CB), BF),
            V((NY - 1, YR, CA), BF), V((NX - 1, YR, CB), BF),
            V((NZH, YR, KVW), BF), V((ROWS, CA), BF), V((ROWS, CB), BF),
            pltpu.SemaphoreType.DMA((6,)), pltpu.SemaphoreType.DMA((D // PW,)),
            dma(6), dma(12), dma(21), dma(7), dma(21), dma(26),
            dma(3), dma(8), dma(7), dma(3), dma(2), dma(7), dma(3), dma(3), dma(7),
        ],
        compiler_params=pltpu.CompilerParams(
            collective_id=0, has_side_effects=True, vmem_limit_bytes=58 << 20
        ),
    )(tokens, queries, keys, targets, weights, m1, m2)


def per_device(
    tokens, queries, rotated_key_rows, targets, value_weights, momentum, first_moment, second_moment
):
    mean = step(
        tokens, queries, rotated_key_rows, targets, value_weights, first_moment[0], second_moment[0]
    )
    mean_direction = mean.astype(F32) + weight_decay * value_weights
    new_momentum = momentum_keep * momentum + mean_direction
    new_weights = value_weights - outer_rate * inner_rate * (
        mean_direction + momentum_keep * new_momentum
    )
    return (new_weights, new_momentum)


def solution(mesh):
    in_specs = (
        P(("rep", "fsdp"), None),
        P(("rep", "fsdp"), None),
        P(("rep", "fsdp"), None),
        P(("rep", "fsdp"), None),
        P("fsdp", None),
        P("fsdp", None),
        P("rep", "fsdp", None),
        P("rep", "fsdp", None),
    )
    out_specs = (P("fsdp", None), P("fsdp", None))
    return jax.shard_map(
        per_device, mesh=mesh, in_specs=in_specs, out_specs=out_specs, check_vma=False
    )
```

```python
import math

import jax
import jax.numpy as jnp
from jax import lax
from jax.experimental import pallas as pl
from jax.experimental.pallas import tpu as pltpu
from jax.sharding import PartitionSpec as P

D = 4096
HEAD = 128
NX, NY, NZH, NZL = 4, 8, 3, 4
NREP = NX * NY * NZH
NF = 8
SEQ = 128
KVW = 512
ROWS = 512
GROUPS = 4
HPG = 4
XR = ROWS // NX
YR = XR // NY
MESH = pl.DeviceIdType.MESH
BF = jnp.bfloat16
F32 = jnp.float32

first_decay = 0.9
second_decay = 0.95
weight_decay = 0.1
inner_rate = 0.05
outer_rate = 0.7
momentum_keep = 0.9
epsilon = 1e-08


def rows(start, size):
    return pl.ds(pl.multiple_of(start, size), size)


HALF = ROWS // 2
RA = ROWS * 3 // 4
XS = RA // NX
YS = (ROWS - RA) // NY
CH = KVW // 2
CA = KVW * 3 // 4
CB = KVW - CA
BR = ROWS // NY
PW = ROWS // 2


def kernel(
    tok_h, q_h, k_h, t_h, w_h, m1_h, m2_h, out_ref,
    tok, q, k, t, w, m1, m2,
    wall, tokc, vgall, probs, acc, dirs, dsend_a, dsend_b,
    recv1a, recv1b, sum_a, sum_b, send_a, send_b, recv2a, recv2b, zbuf, mean_a, mean_b, w_a, w_b, wz_a, wz_b,
    loc, lw, lt, wz, wx, wy, wd, ts, vs, r1a, r1b, r2a, r2b, rz, g1a, g1b, g2a, g2b,
):
    r = lax.axis_index("rep")
    f = lax.axis_index("fsdp")
    zh = lax.div(r, NX * NY)
    x = lax.rem(lax.div(r, NY), NX)
    y = lax.rem(r, NY)
    zl = lax.div(f, 2)
    c = lax.rem(f, 2)

    def dev(zh_=zh, x_=x, y_=y, f_=f):
        return {"rep": zh_ * (NX * NY) + x_ * NY + y_, "fsdp": f_}

    def along(d):
        zp = lax.rem(zh * NZL + zl + d + NZH * NZL, NZH * NZL)
        return dev(zh_=lax.div(zp, NZL), f_=lax.rem(zp, NZL) * 2 + c)

    sib = f + 1 - 2 * c
    sibling = dev(f_=sib)
    right, left, right2, left2 = along(1), along(-1), along(2), along(-2)
    x_r, x_l = dev(x_=lax.rem(x + 1, NX)), dev(x_=lax.rem(x + NX - 1, NX))
    y_r, y_l = dev(y_=lax.rem(y + 1, NY)), dev(y_=lax.rem(y + NY - 1, NY))

    loads = [pltpu.make_async_copy(w_h, w, loc.at[0])]
    at_a, at_b = rows(x * XS, XS), rows(RA + y * YS, YS)
    first = [
        pltpu.make_async_copy(w_h.at[at_a], w_a, lw.at[0]),
        pltpu.make_async_copy(w_h.at[at_b], w_b, lw.at[1]),
    ]
    for cp in first:
        cp.start()
    loads[0].start()

    barrier = pltpu.get_barrier_semaphore()
    peers = [right, left, right2, left2]
    peers += [dev(f_=lax.rem(f + d, NF)) for d in range(1, NF)]
    peers += [dev(x_=lax.rem(x + d, NX)) for d in range(1, NX)]
    peers += [dev(y_=lax.rem(y + d, NY)) for d in range(1, NY)]
    peers += [dev(zh_=lax.rem(zh + d, NZH)) for d in range(1, NZH)]
    for p in peers:
        pl.semaphore_signal(barrier, inc=1, device_id=p, device_id_type=MESH)

    for cp in first:
        cp.wait()
    wz_a[...] = w_a[...].astype(BF)
    wz_b[...] = w_b[...].astype(BF)
    pl.semaphore_wait(barrier, len(peers))

    def remote(src, dst, sem, i, to):
        return pltpu.make_async_remote_copy(
            src_ref=src, dst_ref=dst, send_sem=sem.at[0, i], recv_sem=sem.at[1, i],
            device_id=to, device_id_type=MESH,
        )

    sends = []

    def go(ref, sem, i, to, dst=None):
        cp = remote(ref, ref if dst is None else dst, sem, i, to)
        cp.start()
        sends.append(cp)

    def got(ref, sem, i):
        remote(ref, ref, sem, i, sibling).wait_recv()

    def many(copies, whole, sem, i):
        for src, dst, to in copies:
            remote(src, dst, sem, i, to).start()
        sends.append(remote(whole, whole, sem, i, sibling))

    def flush():
        for cp in sends:
            cp.wait_send()
        sends.clear()

    f_l = lax.rem(zl + NZL - 1, NZL) * 2 + c
    f_r = lax.rem(zl + 1, NZL) * 2 + c
    f_o = lax.rem(zl + 2, NZL) * 2 + c
    slots = [f_l, f_r, f_o]

    def wa(s, p, h=None):
        if h is None:
            return wall.at[s, rows(p * XS, XS)]
        return wall.at[s, rows(p * XS + h * (XS // 2), XS // 2)]

    def wb(s, p):
        return wall.at[s, rows(RA + p * YS, YS)]

    def at_x(d):
        return lax.rem(x + d + NX, NX)

    def at_y(d):
        return lax.rem(y + d + NY, NY)

    far_y = [4, 3, 5, 2, 6, 1, 7]
    far_x = [2, 1, 3]

    go(wz_a, wz, 0, right, dst=wa(f, x))
    go(wz_a, wz, 2, left, dst=wa(f, x))
    go(wz_a, wz, 4, right2, dst=wa(f, x))
    go(wz_b, wz, 5, left2, dst=wb(f, y))
    go(wz_b, wz, 1, right, dst=wb(f, y))
    go(wz_b, wz, 3, left, dst=wb(f, y))
    tloads = []
    for j in range(D // PW):
        ct = pltpu.make_async_copy(tok_h.at[:, pl.ds(j * PW, PW)], tok.at[j], lt.at[j])
        ct.start()
        tloads.append(ct)
    for i, (src, dst) in enumerate([(q_h, q), (k_h, k), (t_h, t), (m1_h, m1), (m2_h, m2)]):
        cp = pltpu.make_async_copy(src, dst, loc.at[i + 1])
        cp.start()
        loads.append(cp)

    loads[0].wait()
    wall[f] = w[...].astype(BF)
    go(wall.at[f], wd, 0, sibling)

    px = lax.div(x, 2)
    pairs = [1 - px, px]
    cuts = [(0, SEQ // 2), (SEQ // 2, SEQ // 2)]

    def tparts(n):
        to = lax.rem(f + n, NF)
        whole = (tok.at[2 * to + pairs[0]], tokc.at[pairs[0], rows(f * SEQ, SEQ)])
        halves = [
            (tok.at[2 * to + pairs[1], pl.ds(at, size)],
             tokc.at[pairs[1], pl.ds(pl.multiple_of(f * SEQ + at, SEQ // 4), size)])
            for at, size in cuts
        ]
        return [whole] + halves

    twhole = [
        tokc.at[0, pl.ds(0, (NF - 1) * SEQ)],
        tokc.at[0, pl.ds(0, (NF - 1) * cuts[0][1])],
        tokc.at[0, pl.ds(0, (NF - 1) * cuts[1][1])],
    ]

    def tsend(part):
        copies = []
        for n in range(1, NF):
            src, dst = tparts(n)[part]
            copies.append((src, dst, dev(f_=lax.rem(f + n, NF))))
        many(copies, twhole[part], ts, part)

    def tgot(part):
        got(twhole[part], ts, part)

    for ct in tloads:
        ct.wait()
    tsend(0)
    tsend(1)
    for m in range(2):
        tokc[m, rows(f * SEQ, SEQ), :] = tok[2 * f + m]

    loads[1].wait()
    loads[2].wait()
    causal = lax.broadcasted_iota(jnp.int32, (SEQ, SEQ), 0) >= lax.broadcasted_iota(
        jnp.int32, (SEQ, SEQ), 1
    )
    score_scale = 1.0 / math.sqrt(HEAD)

    def scores_of(g):
        kg = k[:, g * HEAD : (g + 1) * HEAD]
        for j in range(HPG):
            h = g * HPG + j
            s = lax.dot_general(
                q[:, h * HEAD : (h + 1) * HEAD], kg, (((1,), (1,)), ((), ())),
                preferred_element_type=F32,
            )
            s = jnp.where(causal, s * score_scale, -jnp.inf)
            e = jnp.exp(s - jnp.max(s, axis=-1, keepdims=True))
            p = e / jnp.sum(e, axis=-1, keepdims=True)
            probs[g, j * SEQ : (j + 1) * SEQ, :] = p.astype(BF)

    for g in range(2):
        scores_of(g)

    rest = wall.at[0, pl.ds(0, (NY - 1) * YS)]

    for n, s in enumerate(slots):
        got(wa(s, x), wz, 2 * n)
        go(wa(s, x), wx, n, x_r)
        go(wa(s, x), wx, 3 + n, x_l)
        got(wb(s, y), wz, 2 * n + 1)
        piece = wb(s, y)
        many([(piece, piece, dev(y_=at_y(d))) for d in far_y], rest, wy, n)

    def term(slot, h):
        return jnp.dot(
            tok[2 * slot + h], wall[slot, h * HALF : (h + 1) * HALF, :],
            preferred_element_type=F32,
        )

    for n, s in enumerate(slots):
        got(wa(s, at_x(-1)), wx, n)
        go(wa(s, at_x(-1), 0), wx, 6 + n, x_r)
        got(wa(s, at_x(1)), wx, 3 + n)
        go(wa(s, at_x(1), 1), wx, 9 + n, x_l)
    acc[...] = term(f, 0) + term(f, 1)
    scores_of(2)
    scores_of(3)
    got(wall.at[sib], wd, 0)
    acc[...] += term(sib, 0) + term(sib, 1)

    def part(s, h):
        return wall.at[s, pl.ds(0, RA)] if h == 0 else wall.at[s, pl.ds(RA, ROWS - RA)]

    for n, s in enumerate(slots):
        got(rest, wy, n)
        go(part(s, 1), wd, 4 + n, sibling)
    for n, s in enumerate(slots):
        got(wa(s, at_x(2), 0), wx, 6 + n)
        got(wa(s, at_x(2), 1), wx, 9 + n)
        go(part(s, 0), wd, 1 + n, sibling)
        acc[...] += term(s, 0) + term(s, 1)
    for n, s in enumerate(slots):
        o = s + 1 - 2 * c
        got(part(o, 1), wd, 4 + n)
        got(part(o, 0), wd, 1 + n)
        acc[...] += term(o, 0) + term(o, 1)

    inv_root = 1.0 / math.sqrt(D)
    cot_scale = math.sqrt(D / (SEQ * NF))
    loads[3].wait()

    def value_grad_of(g):
        cols = slice(g * HEAD, (g + 1) * HEAD)
        v = (acc[:, cols] * inv_root).astype(BF)
        o = jnp.dot(probs[g], v, preferred_element_type=F32)
        tg = jnp.concatenate(
            [t[:, (g * HPG + j) * HEAD : (g * HPG + j + 1) * HEAD] for j in range(HPG)], axis=0
        )
        res = ((o - tg.astype(F32)) * cot_scale).astype(BF)
        vg = lax.dot_general(probs[g], res, (((0,), (0,)), ((), ())), preferred_element_type=F32)
        vgall[g // 2, rows(f * SEQ, SEQ), (g % 2) * HEAD : (g % 2 + 1) * HEAD] = vg.astype(BF)

    def vcopy(slot, i, ch, to):
        ref = vgall.at[ch, rows(slot * SEQ, SEQ)]
        return remote(ref, ref, vs, ch * 13 + i, to)

    right_f = dev(f_=jnp.minimum(f + 2, NF - 2 + c))
    left_f = dev(f_=jnp.maximum(f - 2, c))

    def own_copies(ch, act):
        act(vcopy(f, 6, ch, sibling))

        @pl.when(zl < NZL - 1)
        def _():
            act(vcopy(f, 0, ch, right_f))

        @pl.when(zl > 0)
        def _():
            act(vcopy(f, 3, ch, left_f))

    def relay(h, ch, act, wait):
        @pl.when(zl >= h)
        def _():
            slot = f - 2 * h
            if wait:
                vcopy(slot, h - 1, ch, sibling).wait_recv()
            if h < NZL - 1:
                @pl.when(zl < NZL - 1)
                def _():
                    act(vcopy(slot, h, ch, right_f))
            act(vcopy(slot, 6 + h, ch, sibling))

        @pl.when(zl + h < NZL)
        def _():
            slot = f + 2 * h
            if wait:
                vcopy(slot, 3 + h - 1, ch, sibling).wait_recv()
            if h < NZL - 1:
                @pl.when(zl > 0)
                def _():
                    act(vcopy(slot, 3 + h, ch, left_f))
            act(vcopy(slot, 9 + h, ch, sibling))

    def start(cp):
        cp.start()

    def sent(cp):
        cp.wait_send()

    for ch in range(2):
        value_grad_of(2 * ch)
        value_grad_of(2 * ch + 1)
        own_copies(ch, start)
    flush()
    for h in range(1, NZL):
        for ch in range(2):
            relay(h, ch, start, True)
        if h == NZL - 2:
            tsend(2)

    def sibling_got(ch):
        vcopy(sib, 6, ch, sibling).wait_recv()
        for h in range(1, NZL):
            @pl.when(zl >= h)
            def _():
                vcopy(sib - 2 * h, 6 + h, ch, sibling).wait_recv()

            @pl.when(zl + h < NZL)
            def _():
                vcopy(sib + 2 * h, 9 + h, ch, sibling).wait_recv()

    for ch in range(2):
        sibling_got(ch)
    loads[4].wait()
    loads[5].wait()

    A, B = slice(0, CA), slice(CA, KVW)

    def direction(m, e):
        n = 2 * m + e
        at = rows(n * XR, XR)
        for ch in range(2):
            cols = slice(ch * CH, (ch + 1) * CH)
            grad = lax.dot_general(
                tokc[m, :, rows(e * XR, XR)], vgall[ch], (((0,), (0,)), ((), ())),
                preferred_element_type=F32,
            ) * inv_root
            fn = first_decay * m1[at, cols] + (1.0 - first_decay) * grad
            sn = second_decay * m2[at, cols] + (1.0 - second_decay) * grad * grad
            dirs[at, cols] = fn / (jnp.sqrt(sn) + epsilon)
        d = dirs[at, :]
        dsend_a[at, :] = d[:, A].astype(BF)
        dsend_b[at, :] = d[:, B].astype(BF)
        return n

    b = lax.rem(x, 2)
    for i, (m, e) in enumerate([(1 - px, b), (1 - px, 1 - b), (px, 1 - b), (px, b)]):
        if i == 0:
            tgot(0)
        if i == 2:
            tgot(1)
            tgot(2)
        n = direction(m, e)
        if i < 3:
            go(dsend_a.at[rows(n * XR, XR)], r1a, i, dev(x_=n), dst=recv1a.at[i])
        for u in range(2):
            to = 2 * n + u
            j = lax.rem(to - y + NY, NY)
            cp = remote(dsend_b.at[rows(to * BR, BR)], recv1b.at[j], r1b, 0, dev(y_=to))

            @pl.when(to != y)
            def _():
                cp.start()

    b_whole = recv1b.at[pl.ds(0, NY - 1)]
    sends.append(remote(b_whole, b_whole, r1b, 0, sibling))
    for ch in range(2):
        own_copies(ch, sent)
        for h in range(1, NZL):
            relay(h, ch, sent, False)
    for i in range(3):
        got(recv1a.at[i], r1a, i)
    total = dirs[rows(x * XR, XR), A]
    for i in range(3):
        total = total + recv1a[i].astype(F32)
    sum_a[...] = total
    send_a[...] = total.astype(BF)
    many(
        [(send_a.at[rows(at_y(d) * YR, YR)], recv2a.at[d - 1], dev(y_=at_y(d))) for d in far_y],
        recv2a, r2a, 0,
    )
    got(b_whole, r1b, 0)
    total = dirs[rows(y * BR, BR), B]
    for d in range(1, NY):
        total = total + recv1b[d].astype(F32)
    sum_b[...] = total
    send_b[...] = total.astype(BF)
    late = list(sends)
    sends.clear()
    many(
        [(send_b.at[rows(at_x(d) * YR, YR)], recv2b.at[d - 1], dev(x_=at_x(d))) for d in far_x],
        recv2b, r2b, 0,
    )
    for cp in late:
        cp.wait_send()
    got(recv2a, r2a, 0)
    total = sum_a[rows(y * YR, YR), :]
    for d in range(1, NY):
        total = total + recv2a[d - 1].astype(F32)
    zbuf[zh, :, A] = total.astype(BF)
    got(recv2b, r2b, 0)
    total = sum_b[rows(x * YR, YR), :]
    for d in range(1, NX):
        total = total + recv2b[d - 1].astype(F32)
    zbuf[zh, :, B] = total.astype(BF)

    late = list(sends)
    sends.clear()
    for d in range(1, NZH):
        go(zbuf.at[zh], rz, d - 1, dev(zh_=lax.rem(zh + d, NZH)))
    for cp in late:
        cp.wait_send()
    for d in range(1, NZH):
        got(zbuf.at[lax.rem(zh + NZH - d, NZH)], rz, d - 1)

    def spot_a(x_, y_):
        return mean_a.at[rows(x_ * XR + y_ * YR, YR)]

    def spot_b(x_, y_):
        return mean_b.at[rows(y_ * BR + x_ * YR, YR)]

    total = zbuf[0].astype(F32)
    for z in range(1, NZH):
        total = total + zbuf[z].astype(F32)
    piece = (total * (1.0 / NREP)).astype(BF)
    mean_a[rows(x * XR + y * YR, YR), :] = piece[:, A]
    a7, a3 = mean_a.at[pl.ds(0, (NY - 1) * YR)], mean_a.at[pl.ds(0, (NX - 1) * XR)]
    b3, b7 = mean_b.at[pl.ds(0, (NX - 1) * YR)], mean_b.at[pl.ds(0, (NY - 1) * BR)]
    spot = spot_a(x, y)
    many([(spot, spot, dev(y_=at_y(d))) for d in far_y], a7, g1a, 0)
    mean_b[rows(y * BR + x * YR, YR), :] = piece[:, B]
    spot = spot_b(x, y)
    many([(spot, spot, dev(x_=at_x(d))) for d in far_x], b3, g1b, 0)
    got(b3, g1b, 0)
    block = mean_b.at[rows(y * BR, BR)]
    many([(block, block, dev(y_=at_y(d))) for d in far_y], b7, g2b, 0)
    got(a7, g1a, 0)
    block = mean_a.at[rows(x * XR, XR)]
    many([(block, block, dev(x_=at_x(d))) for d in far_x], a3, g2a, 0)
    flush()
    got(b7, g2b, 0)
    out_ref[:, B] = mean_b[...]
    got(a3, g2a, 0)
    out_ref[:, A] = mean_a[...]


def step(tokens, queries, keys, targets, weights, m1, m2):
    def dma(n):
        return pltpu.SemaphoreType.DMA((2, n))

    V = pltpu.VMEM
    return pl.pallas_call(
        kernel,
        out_shape=jax.ShapeDtypeStruct((ROWS, KVW), BF),
        in_specs=[pl.BlockSpec(memory_space=pl.ANY)] * 7,
        out_specs=pl.BlockSpec(memory_space=pltpu.VMEM),
        scratch_shapes=[
            V((D // PW, SEQ, PW), BF), V((SEQ, 2048), BF), V((SEQ, KVW), BF), V((SEQ, 2048), BF),
            V((ROWS, KVW), F32), V((ROWS, KVW), F32), V((ROWS, KVW), F32),
            V((NF, ROWS, KVW), BF), V((2, NF * SEQ, PW), BF), V((2, NF * SEQ, CH), BF),
            V((GROUPS, HPG * SEQ, SEQ), BF), V((SEQ, KVW), F32),
            V((ROWS, KVW), F32), V((ROWS, CA), BF), V((ROWS, CB), BF),
            V((NX - 1, XR, CA), BF), V((NY, BR, CB), BF),
            V((XR, CA), F32), V((BR, CB), F32), V((XR, CA), BF), V((BR, CB), BF),
            V((NY - 1, YR, CA), BF), V((NX - 1, YR, CB), BF),
            V((NZH, YR, KVW), BF), V((ROWS, CA), BF), V((ROWS, CB), BF),
            V((XS, KVW), F32), V((YS, KVW), F32), V((XS, KVW), BF), V((YS, KVW), BF),
            pltpu.SemaphoreType.DMA((6,)), pltpu.SemaphoreType.DMA((2,)), pltpu.SemaphoreType.DMA((D // PW,)),
            dma(6), dma(12), dma(3), dma(7), dma(3), dma(26),
            dma(3), dma(1), dma(1), dma(1), dma(2), dma(1), dma(1), dma(1), dma(1),
        ],
        compiler_params=pltpu.CompilerParams(
            collective_id=0, has_side_effects=True, vmem_limit_bytes=58 << 20
        ),
    )(tokens, queries, keys, targets, weights, m1, m2)


def per_device(
    tokens, queries, rotated_key_rows, targets, value_weights, momentum, first_moment, second_moment
):
    mean = step(
        tokens, queries, rotated_key_rows, targets, value_weights, first_moment[0], second_moment[0]
    )
    mean_direction = mean.astype(F32) + weight_decay * value_weights
    new_momentum = momentum_keep * momentum + mean_direction
    new_weights = value_weights - outer_rate * inner_rate * (
        mean_direction + momentum_keep * new_momentum
    )
    return (new_weights, new_momentum)


def solution(mesh):
    in_specs = (
        P(("rep", "fsdp"), None),
        P(("rep", "fsdp"), None),
        P(("rep", "fsdp"), None),
        P(("rep", "fsdp"), None),
        P("fsdp", None),
        P("fsdp", None),
        P("rep", "fsdp", None),
        P("rep", "fsdp", None),
    )
    out_specs = (P("fsdp", None), P("fsdp", None))
    return jax.shard_map(
        per_device, mesh=mesh, in_specs=in_specs, out_specs=out_specs, check_vma=False
    )
```

```python
import math

import jax
import jax.numpy as jnp
from jax import lax
from jax.experimental import pallas as pl
from jax.experimental.pallas import tpu as pltpu
from jax.sharding import PartitionSpec as P

D = 4096
HEAD = 128
NX, NY, NZH, NZL = 4, 8, 3, 4
NREP = NX * NY * NZH
NF = 8
SEQ = 128
KVW = 512
ROWS = 512
GROUPS = 4
HPG = 4
XR = ROWS // NX
YR = XR // NY
MESH = pl.DeviceIdType.MESH
BF = jnp.bfloat16
F32 = jnp.float32

first_decay = 0.9
second_decay = 0.95
weight_decay = 0.1
inner_rate = 0.05
outer_rate = 0.7
momentum_keep = 0.9
epsilon = 1e-08


def rows(start, size):
    return pl.ds(pl.multiple_of(start, size), size)


HALF = ROWS // 2
RA = ROWS * 3 // 4
XS = RA // NX
YS = (ROWS - RA) // NY
CH = KVW // 2
CA = KVW * 3 // 4
CB = KVW - CA
BR = ROWS // NY
PW = ROWS // 2


def kernel(
    tok_h, q_h, k_h, t_h, w_h, m1_h, m2_h, out_ref,
    tok, q, k, t, w, m1, m2,
    wall, tokc, vgall, probs, acc, dirs, dsend_a, dsend_b,
    recv1a, recv1b, sum_a, sum_b, send_a, send_b, recv2a, recv2b, zbuf, mean_a, mean_b, w_a, w_b, wz_a, wz_b,
    loc, lw, lt, wz, wx, wy, wd, ts, vs, r1a, r1b, r2a, r2b, rz, g1a, g1b, g2a, g2b,
):
    r = lax.axis_index("rep")
    f = lax.axis_index("fsdp")
    zh = lax.div(r, NX * NY)
    x = lax.rem(lax.div(r, NY), NX)
    y = lax.rem(r, NY)
    zl = lax.div(f, 2)
    c = lax.rem(f, 2)

    def dev(zh_=zh, x_=x, y_=y, f_=f):
        return {"rep": zh_ * (NX * NY) + x_ * NY + y_, "fsdp": f_}

    def along(d):
        zp = lax.rem(zh * NZL + zl + d + NZH * NZL, NZH * NZL)
        return dev(zh_=lax.div(zp, NZL), f_=lax.rem(zp, NZL) * 2 + c)

    sib = f + 1 - 2 * c
    sibling = dev(f_=sib)
    right, left, right2, left2 = along(1), along(-1), along(2), along(-2)
    x_r, x_l = dev(x_=lax.rem(x + 1, NX)), dev(x_=lax.rem(x + NX - 1, NX))
    y_r, y_l = dev(y_=lax.rem(y + 1, NY)), dev(y_=lax.rem(y + NY - 1, NY))

    loads = [pltpu.make_async_copy(w_h, w, loc.at[0])]
    at_a, at_b = rows(x * XS, XS), rows(RA + y * YS, YS)
    first = [
        pltpu.make_async_copy(w_h.at[at_a], w_a, lw.at[0]),
        pltpu.make_async_copy(w_h.at[at_b], w_b, lw.at[1]),
    ]
    for cp in first:
        cp.start()
    loads[0].start()

    barrier = pltpu.get_barrier_semaphore()
    peers = [right, left, right2, left2]
    peers += [dev(f_=lax.rem(f + d, NF)) for d in range(1, NF)]
    peers += [dev(x_=lax.rem(x + d, NX)) for d in range(1, NX)]
    peers += [dev(y_=lax.rem(y + d, NY)) for d in range(1, NY)]
    peers += [dev(zh_=lax.rem(zh + d, NZH)) for d in range(1, NZH)]
    for p in peers:
        pl.semaphore_signal(barrier, inc=1, device_id=p, device_id_type=MESH)

    for cp in first:
        cp.wait()
    wz_a[...] = w_a[...].astype(BF)
    wz_b[...] = w_b[...].astype(BF)
    pl.semaphore_wait(barrier, len(peers))

    def remote(src, dst, sem, i, to):
        return pltpu.make_async_remote_copy(
            src_ref=src, dst_ref=dst, send_sem=sem.at[0, i], recv_sem=sem.at[1, i],
            device_id=to, device_id_type=MESH,
        )

    sends = []

    def go(ref, sem, i, to, dst=None):
        cp = remote(ref, ref if dst is None else dst, sem, i, to)
        cp.start()
        sends.append(cp)

    def got(ref, sem, i):
        remote(ref, ref, sem, i, sibling).wait_recv()

    def many(copies, whole, sem, i):
        for src, dst, to in copies:
            remote(src, dst, sem, i, to).start()
        sends.append(remote(whole, whole, sem, i, sibling))

    def flush():
        for cp in sends:
            cp.wait_send()
        sends.clear()

    f_l = lax.rem(zl + NZL - 1, NZL) * 2 + c
    f_r = lax.rem(zl + 1, NZL) * 2 + c
    f_o = lax.rem(zl + 2, NZL) * 2 + c
    slots = [f_l, f_r, f_o]

    def wa(s, p, h=None):
        if h is None:
            return wall.at[s, rows(p * XS, XS)]
        return wall.at[s, rows(p * XS + h * (XS // 2), XS // 2)]

    def wb(s, p):
        return wall.at[s, rows(RA + p * YS, YS)]

    def at_x(d):
        return lax.rem(x + d + NX, NX)

    def at_y(d):
        return lax.rem(y + d + NY, NY)

    far_y = [4, 3, 5, 2, 6, 1, 7]
    far_x = [2, 1, 3]

    go(wz_a, wz, 0, right, dst=wa(f, x))
    go(wz_a, wz, 2, left, dst=wa(f, x))
    go(wz_a, wz, 4, right2, dst=wa(f, x))
    go(wz_b, wz, 5, left2, dst=wb(f, y))
    go(wz_b, wz, 1, right, dst=wb(f, y))
    go(wz_b, wz, 3, left, dst=wb(f, y))
    tloads = []
    for j in range(D // PW):
        ct = pltpu.make_async_copy(tok_h.at[:, pl.ds(j * PW, PW)], tok.at[j], lt.at[j])
        ct.start()
        tloads.append(ct)
    for i, (src, dst) in enumerate([(q_h, q), (k_h, k), (t_h, t), (m1_h, m1), (m2_h, m2)]):
        cp = pltpu.make_async_copy(src, dst, loc.at[i + 1])
        cp.start()
        loads.append(cp)

    loads[0].wait()
    wall[f] = w[...].astype(BF)
    go(wall.at[f], wd, 0, sibling)

    px = lax.div(x, 2)
    pairs = [1 - px, px]
    cuts = [(0, SEQ // 2), (SEQ // 2, SEQ // 2)]

    def tparts(n):
        to = lax.rem(f + n, NF)
        whole = (tok.at[2 * to + pairs[0]], tokc.at[pairs[0], rows(f * SEQ, SEQ)])
        halves = [
            (tok.at[2 * to + pairs[1], pl.ds(at, size)],
             tokc.at[pairs[1], pl.ds(pl.multiple_of(f * SEQ + at, SEQ // 4), size)])
            for at, size in cuts
        ]
        return [whole] + halves

    twhole = [
        tokc.at[0, pl.ds(0, (NF - 1) * SEQ)],
        tokc.at[0, pl.ds(0, (NF - 1) * cuts[0][1])],
        tokc.at[0, pl.ds(0, (NF - 1) * cuts[1][1])],
    ]

    def tsend(part):
        copies = []
        for n in range(1, NF):
            src, dst = tparts(n)[part]
            copies.append((src, dst, dev(f_=lax.rem(f + n, NF))))
        many(copies, twhole[part], ts, part)

    def tgot(part):
        got(twhole[part], ts, part)

    for ct in tloads:
        ct.wait()
    tsend(0)
    tsend(1)
    for m in range(2):
        tokc[m, rows(f * SEQ, SEQ), :] = tok[2 * f + m]

    loads[1].wait()
    loads[2].wait()
    causal = lax.broadcasted_iota(jnp.int32, (SEQ, SEQ), 0) >= lax.broadcasted_iota(
        jnp.int32, (SEQ, SEQ), 1
    )
    score_scale = 1.0 / math.sqrt(HEAD)

    def scores_of(g):
        kg = k[:, g * HEAD : (g + 1) * HEAD]
        for j in range(HPG):
            h = g * HPG + j
            s = lax.dot_general(
                q[:, h * HEAD : (h + 1) * HEAD], kg, (((1,), (1,)), ((), ())),
                preferred_element_type=F32,
            )
            s = jnp.where(causal, s * score_scale, -jnp.inf)
            e = jnp.exp(s - jnp.max(s, axis=-1, keepdims=True))
            p = e / jnp.sum(e, axis=-1, keepdims=True)
            probs[g, j * SEQ : (j + 1) * SEQ, :] = p.astype(BF)

    for g in range(2):
        scores_of(g)

    rest = wall.at[0, pl.ds(0, (NY - 1) * YS)]

    def hand(s, n, d):
        piece = wa(s, at_x(d))
        remote(piece, piece, wd, 1 + n, sibling).start()

    for n, s in enumerate(slots):
        got(wa(s, x), wz, 2 * n)
        go(wa(s, x), wx, n, x_r)
        go(wa(s, x), wx, 3 + n, x_l)
        hand(s, n, 0)
        got(wb(s, y), wz, 2 * n + 1)
        piece = wb(s, y)
        many([(piece, piece, dev(y_=at_y(d))) for d in far_y], rest, wy, n)

    def term(slot, h):
        return jnp.dot(
            tok[2 * slot + h], wall[slot, h * HALF : (h + 1) * HALF, :],
            preferred_element_type=F32,
        )

    for n, s in enumerate(slots):
        got(wa(s, at_x(-1)), wx, n)
        go(wa(s, at_x(-1), 0), wx, 6 + n, x_r)
        hand(s, n, -1)
        got(wa(s, at_x(1)), wx, 3 + n)
        go(wa(s, at_x(1), 1), wx, 9 + n, x_l)
        hand(s, n, 1)
    acc[...] = term(f, 0) + term(f, 1)
    scores_of(2)
    scores_of(3)
    got(wall.at[sib], wd, 0)
    acc[...] += term(sib, 0) + term(sib, 1)

    def part(s, h):
        return wall.at[s, pl.ds(0, RA)] if h == 0 else wall.at[s, pl.ds(RA, ROWS - RA)]

    for n, s in enumerate(slots):
        got(rest, wy, n)
        go(part(s, 1), wd, 4 + n, sibling)
    for n, s in enumerate(slots):
        got(wa(s, at_x(2), 0), wx, 6 + n)
        got(wa(s, at_x(2), 1), wx, 9 + n)
        hand(s, n, 2)
        sends.append(remote(part(s, 0), part(s, 0), wd, 1 + n, sibling))
        acc[...] += term(s, 0) + term(s, 1)
    for n, s in enumerate(slots):
        o = s + 1 - 2 * c
        got(part(o, 1), wd, 4 + n)
        got(part(o, 0), wd, 1 + n)
        acc[...] += term(o, 0) + term(o, 1)

    inv_root = 1.0 / math.sqrt(D)
    cot_scale = math.sqrt(D / (SEQ * NF))
    loads[3].wait()

    def value_grad_of(g):
        cols = slice(g * HEAD, (g + 1) * HEAD)
        v = (acc[:, cols] * inv_root).astype(BF)
        o = jnp.dot(probs[g], v, preferred_element_type=F32)
        tg = jnp.concatenate(
            [t[:, (g * HPG + j) * HEAD : (g * HPG + j + 1) * HEAD] for j in range(HPG)], axis=0
        )
        res = ((o - tg.astype(F32)) * cot_scale).astype(BF)
        vg = lax.dot_general(probs[g], res, (((0,), (0,)), ((), ())), preferred_element_type=F32)
        vgall[g // 2, rows(f * SEQ, SEQ), (g % 2) * HEAD : (g % 2 + 1) * HEAD] = vg.astype(BF)

    def vcopy(slot, i, ch, to):
        ref = vgall.at[ch, rows(slot * SEQ, SEQ)]
        return remote(ref, ref, vs, ch * 13 + i, to)

    right_f = dev(f_=jnp.minimum(f + 2, NF - 2 + c))
    left_f = dev(f_=jnp.maximum(f - 2, c))

    def own_copies(ch, act):
        act(vcopy(f, 6, ch, sibling))

        @pl.when(zl < NZL - 1)
        def _():
            act(vcopy(f, 0, ch, right_f))

        @pl.when(zl > 0)
        def _():
            act(vcopy(f, 3, ch, left_f))

    def relay(h, ch, act, wait):
        @pl.when(zl >= h)
        def _():
            slot = f - 2 * h
            if wait:
                vcopy(slot, h - 1, ch, sibling).wait_recv()
            if h < NZL - 1:
                @pl.when(zl < NZL - 1)
                def _():
                    act(vcopy(slot, h, ch, right_f))
            act(vcopy(slot, 6 + h, ch, sibling))

        @pl.when(zl + h < NZL)
        def _():
            slot = f + 2 * h
            if wait:
                vcopy(slot, 3 + h - 1, ch, sibling).wait_recv()
            if h < NZL - 1:
                @pl.when(zl > 0)
                def _():
                    act(vcopy(slot, 3 + h, ch, left_f))
            act(vcopy(slot, 9 + h, ch, sibling))

    def start(cp):
        cp.start()

    def sent(cp):
        cp.wait_send()

    for ch in range(2):
        value_grad_of(2 * ch)
        value_grad_of(2 * ch + 1)
        own_copies(ch, start)
    flush()
    for h in range(1, NZL):
        for ch in range(2):
            relay(h, ch, start, True)
        if h == NZL - 2:
            tsend(2)

    def sibling_got(ch):
        vcopy(sib, 6, ch, sibling).wait_recv()
        for h in range(1, NZL):
            @pl.when(zl >= h)
            def _():
                vcopy(sib - 2 * h, 6 + h, ch, sibling).wait_recv()

            @pl.when(zl + h < NZL)
            def _():
                vcopy(sib + 2 * h, 9 + h, ch, sibling).wait_recv()

    for ch in range(2):
        sibling_got(ch)
    loads[4].wait()
    loads[5].wait()

    A, B = slice(0, CA), slice(CA, KVW)

    def direction(m, e):
        n = 2 * m + e
        at = rows(n * XR, XR)
        for ch in range(2):
            cols = slice(ch * CH, (ch + 1) * CH)
            grad = lax.dot_general(
                tokc[m, :, rows(e * XR, XR)], vgall[ch], (((0,), (0,)), ((), ())),
                preferred_element_type=F32,
            ) * inv_root
            fn = first_decay * m1[at, cols] + (1.0 - first_decay) * grad
            sn = second_decay * m2[at, cols] + (1.0 - second_decay) * grad * grad
            dirs[at, cols] = fn / (jnp.sqrt(sn) + epsilon)
        d = dirs[at, :]
        dsend_a[at, :] = d[:, A].astype(BF)
        dsend_b[at, :] = d[:, B].astype(BF)
        return n

    b = lax.rem(x, 2)
    for i, (m, e) in enumerate([(1 - px, b), (1 - px, 1 - b), (px, 1 - b), (px, b)]):
        if i == 0:
            tgot(0)
        if i == 2:
            tgot(1)
            tgot(2)
        n = direction(m, e)
        if i < 3:
            go(dsend_a.at[rows(n * XR, XR)], r1a, i, dev(x_=n), dst=recv1a.at[i])
        for u in range(2):
            to = 2 * n + u
            j = lax.rem(to - y + NY, NY)
            cp = remote(dsend_b.at[rows(to * BR, BR)], recv1b.at[j], r1b, 0, dev(y_=to))

            @pl.when(to != y)
            def _():
                cp.start()

    b_whole = recv1b.at[pl.ds(0, NY - 1)]
    sends.append(remote(b_whole, b_whole, r1b, 0, sibling))
    for ch in range(2):
        own_copies(ch, sent)
        for h in range(1, NZL):
            relay(h, ch, sent, False)
    for i in range(3):
        got(recv1a.at[i], r1a, i)
    total = dirs[rows(x * XR, XR), A]
    for i in range(3):
        total = total + recv1a[i].astype(F32)
    sum_a[...] = total
    send_a[...] = total.astype(BF)
    many(
        [(send_a.at[rows(at_y(d) * YR, YR)], recv2a.at[d - 1], dev(y_=at_y(d))) for d in far_y],
        recv2a, r2a, 0,
    )
    got(b_whole, r1b, 0)
    total = dirs[rows(y * BR, BR), B]
    for d in range(1, NY):
        total = total + recv1b[d].astype(F32)
    sum_b[...] = total
    send_b[...] = total.astype(BF)
    late = list(sends)
    sends.clear()
    many(
        [(send_b.at[rows(at_x(d) * YR, YR)], recv2b.at[d - 1], dev(x_=at_x(d))) for d in far_x],
        recv2b, r2b, 0,
    )
    for cp in late:
        cp.wait_send()
    got(recv2a, r2a, 0)
    total = sum_a[rows(y * YR, YR), :]
    for d in range(1, NY):
        total = total + recv2a[d - 1].astype(F32)
    zbuf[zh, :, A] = total.astype(BF)
    got(recv2b, r2b, 0)
    total = sum_b[rows(x * YR, YR), :]
    for d in range(1, NX):
        total = total + recv2b[d - 1].astype(F32)
    zbuf[zh, :, B] = total.astype(BF)

    late = list(sends)
    sends.clear()
    for d in range(1, NZH):
        go(zbuf.at[zh], rz, d - 1, dev(zh_=lax.rem(zh + d, NZH)))
    for cp in late:
        cp.wait_send()
    for d in range(1, NZH):
        got(zbuf.at[lax.rem(zh + NZH - d, NZH)], rz, d - 1)

    def spot_a(x_, y_):
        return mean_a.at[rows(x_ * XR + y_ * YR, YR)]

    def spot_b(x_, y_):
        return mean_b.at[rows(y_ * BR + x_ * YR, YR)]

    total = zbuf[0].astype(F32)
    for z in range(1, NZH):
        total = total + zbuf[z].astype(F32)
    piece = (total * (1.0 / NREP)).astype(BF)
    mean_a[rows(x * XR + y * YR, YR), :] = piece[:, A]
    a7, a3 = mean_a.at[pl.ds(0, (NY - 1) * YR)], mean_a.at[pl.ds(0, (NX - 1) * XR)]
    b3, b7 = mean_b.at[pl.ds(0, (NX - 1) * YR)], mean_b.at[pl.ds(0, (NY - 1) * BR)]
    spot = spot_a(x, y)
    many([(spot, spot, dev(y_=at_y(d))) for d in far_y], a7, g1a, 0)
    mean_b[rows(y * BR + x * YR, YR), :] = piece[:, B]
    spot = spot_b(x, y)
    many([(spot, spot, dev(x_=at_x(d))) for d in far_x], b3, g1b, 0)
    got(b3, g1b, 0)
    block = mean_b.at[rows(y * BR, BR)]
    many([(block, block, dev(y_=at_y(d))) for d in far_y], b7, g2b, 0)
    got(a7, g1a, 0)
    block = mean_a.at[rows(x * XR, XR)]
    many([(block, block, dev(x_=at_x(d))) for d in far_x], a3, g2a, 0)
    flush()
    got(b7, g2b, 0)
    out_ref[:, B] = mean_b[...]
    got(a3, g2a, 0)
    out_ref[:, A] = mean_a[...]


def step(tokens, queries, keys, targets, weights, m1, m2):
    def dma(n):
        return pltpu.SemaphoreType.DMA((2, n))

    V = pltpu.VMEM
    return pl.pallas_call(
        kernel,
        out_shape=jax.ShapeDtypeStruct((ROWS, KVW), BF),
        in_specs=[pl.BlockSpec(memory_space=pl.ANY)] * 7,
        out_specs=pl.BlockSpec(memory_space=pltpu.VMEM),
        scratch_shapes=[
            V((D // PW, SEQ, PW), BF), V((SEQ, 2048), BF), V((SEQ, KVW), BF), V((SEQ, 2048), BF),
            V((ROWS, KVW), F32), V((ROWS, KVW), F32), V((ROWS, KVW), F32),
            V((NF, ROWS, KVW), BF), V((2, NF * SEQ, PW), BF), V((2, NF * SEQ, CH), BF),
            V((GROUPS, HPG * SEQ, SEQ), BF), V((SEQ, KVW), F32),
            V((ROWS, KVW), F32), V((ROWS, CA), BF), V((ROWS, CB), BF),
            V((NX - 1, XR, CA), BF), V((NY, BR, CB), BF),
            V((XR, CA), F32), V((BR, CB), F32), V((XR, CA), BF), V((BR, CB), BF),
            V((NY - 1, YR, CA), BF), V((NX - 1, YR, CB), BF),
            V((NZH, YR, KVW), BF), V((ROWS, CA), BF), V((ROWS, CB), BF),
            V((XS, KVW), F32), V((YS, KVW), F32), V((XS, KVW), BF), V((YS, KVW), BF),
            pltpu.SemaphoreType.DMA((6,)), pltpu.SemaphoreType.DMA((2,)), pltpu.SemaphoreType.DMA((D // PW,)),
            dma(6), dma(12), dma(3), dma(7), dma(3), dma(26),
            dma(3), dma(1), dma(1), dma(1), dma(2), dma(1), dma(1), dma(1), dma(1),
        ],
        compiler_params=pltpu.CompilerParams(
            collective_id=0, has_side_effects=True, vmem_limit_bytes=58 << 20
        ),
    )(tokens, queries, keys, targets, weights, m1, m2)


def per_device(
    tokens, queries, rotated_key_rows, targets, value_weights, momentum, first_moment, second_moment
):
    mean = step(
        tokens, queries, rotated_key_rows, targets, value_weights, first_moment[0], second_moment[0]
    )
    mean_direction = mean.astype(F32) + weight_decay * value_weights
    new_momentum = momentum_keep * momentum + mean_direction
    new_weights = value_weights - outer_rate * inner_rate * (
        mean_direction + momentum_keep * new_momentum
    )
    return (new_weights, new_momentum)


def solution(mesh):
    in_specs = (
        P(("rep", "fsdp"), None),
        P(("rep", "fsdp"), None),
        P(("rep", "fsdp"), None),
        P(("rep", "fsdp"), None),
        P("fsdp", None),
        P("fsdp", None),
        P("rep", "fsdp", None),
        P("rep", "fsdp", None),
    )
    out_specs = (P("fsdp", None), P("fsdp", None))
    return jax.shard_map(
        per_device, mesh=mesh, in_specs=in_specs, out_specs=out_specs, check_vma=False
    )
```
